256 devices in a mesh: item: 16 (over y, x_lo, core), feat: 16 (over x_hi, z).
Axes of the slice: x: 4 (x_hi: 2, x_lo: 2; x = x_hi * 2 + x_lo), y: 4, z: 8, core: 2. Of those that a mesh axis runs over, the one named last changes fastest.
Arguments:
- teacher: bfloat16 [32768, 4096], P('item', 'feat'), may hold values from -16 to 16
- codebooks: bfloat16 [4, 256, 512], replicated, may hold values from -3 to 3
- codes: int32 [32768, 4], P(('item', 'feat')), may hold values from 0 to 255, as said below
Outputs:
- loss: float32 [], replicated
- codebook_grad: float32 [4, 256, 512], replicated
The draws below stay inside these ranges and needn't reach their ends.
Inputs may be any that keep to these rules, and one draw needn't show every extreme that they name: codes index the rows of their level's codebook. Let q be an item's index divided by 128, w = 1 and h = 128. An item's level-0 code is q * w + r modulo 256, and its level-1 code is (q modulo h) * 2 * w + r' modulo 256, with r and r' from 0 to 2 * w - 1; the other levels' codes are unrestricted.
All inputs are finite; a program needn't handle non-finite values.
Results may differ from the reference program's by a relative error of at most 0.0065.
Values may be sent and summed in bfloat16 or wider, within the bound.
No kernel may reach another device: no remote copies, remote signals or barrier semaphores. Data moves between devices by JAX's collectives and lax.ppermute only.
A program may use at most 64 MiB of HBM per device.

```python
import math
import jax
import jax.numpy as jnp
from jax import lax

DS = 512
DT = 4096
LEVELS = 4
CODES = 256
ROWS_DEV = 128
ITEMS = 32768
N_FEAT = 16


def shared_codes(key):
    device_total = ITEMS // ROWS_DEV
    window = CODES // device_total
    half_total = max(device_total // 2, 1)
    base_key = jax.random.fold_in(key, 7)
    device = (jnp.arange(ITEMS, dtype=jnp.int32) // ROWS_DEV).astype(jnp.int32)
    random_codes = jax.random.randint(base_key, (ITEMS, LEVELS), 0, CODES, dtype=jnp.int32)
    offset_first = jax.random.randint(jax.random.fold_in(base_key, 1), (ITEMS,), 0, 2 * window, dtype=jnp.int32)
    offset_second = jax.random.randint(jax.random.fold_in(base_key, 2), (ITEMS,), 0, 2 * window, dtype=jnp.int32)
    first = (device * window + offset_first) % CODES
    second = (device % half_total * 2 * window + offset_second) % CODES
    return jnp.concatenate([first[:, None], second[:, None], random_codes[:, 2:]], axis=1).astype(jnp.int32)


def draw_codes(key, part):
    return shared_codes(key)


def draw_teacher(key, part):
    code_table = shared_codes(key)
    table_key = jax.random.fold_in(key, 19)
    tables = jax.random.normal(table_key, (LEVELS, CODES, DT), jnp.float32)
    common = jnp.zeros((ITEMS, DT), jnp.float32)
    for level in range(LEVELS):
        common = common + 0.5 * jnp.take(tables[level], code_table[:, level], axis=0)
    position = jnp.arange(DT, dtype=jnp.float32) / float(max(DT - 1, 1))
    noise = 0.6 * jax.random.normal(jax.random.fold_in(table_key, 1), (ITEMS, DT), jnp.float32)
    growth = math.log(3.0)
    values = (common + noise) * jnp.exp(position * growth)[None, :]
    return jnp.clip(values, -16.0, 16.0).astype(jnp.bfloat16)


def normal_values(key, shape, spread, bound, kind=jnp.bfloat16):
    entries = spread * jax.random.normal(key, shape, jnp.float32)
    return jnp.clip(entries, min=-bound, max=bound).astype(kind)


def setup_inputs(seed: int = 0) -> dict:
    key_of = jax.random.split(jax.random.key(seed), 4)
    teacher = draw_teacher(jax.random.fold_in(key_of[3], 71), 0)
    codebooks = normal_values(key_of[1], (LEVELS, CODES, DS), 0.5, 3.0)
    codes = draw_codes(jax.random.fold_in(key_of[3], 71), 0)
    return {"teacher": teacher, "codebooks": codebooks, "codes": codes}


epsilon = 1e-06

def rebuild(codes, codebooks):
    recon = jnp.zeros((codes.shape[0], codebooks.shape[2]), jnp.float32)
    for level in range(codebooks.shape[0]):
        recon = recon + jnp.take(codebooks[level], codes[:, level], axis=0).astype(jnp.float32)
    inv = lax.rsqrt(lax.optimization_barrier(jnp.mean(recon * recon, axis=-1, keepdims=True)) + epsilon)
    return (recon * inv, inv)

def reference(teacher, codebooks, codes):
    tfull = teacher.astype(jnp.float32)
    squares = lax.optimization_barrier(jnp.sum(tfull * tfull, axis=-1, keepdims=True))
    tnorm = (tfull * lax.rsqrt(squares / DT + epsilon)).astype(jnp.bfloat16)
    s_full, inv = rebuild(codes, codebooks)
    student = s_full.astype(jnp.bfloat16)
    cross = jnp.dot(tnorm.T, student, preferred_element_type=jnp.float32)
    gram = jnp.dot(student.T, student, preferred_element_type=jnp.float32)
    scale = float(ITEMS) * float(ITEMS) * float(DS)
    loss = (jnp.sum(gram * gram) - 2.0 * jnp.sum(cross * cross)) / scale
    cross_b = cross.astype(jnp.bfloat16)
    gram_b = gram.astype(jnp.bfloat16)
    width = DT // N_FEAT

    def add_block(total, block):
        start = (block * width).astype(jnp.int32)
        rows = lax.dynamic_slice_in_dim(tnorm, start, width, 1)
        weights = lax.dynamic_slice_in_dim(cross_b, start, width, 0)
        part = jnp.dot(rows, weights, preferred_element_type=jnp.float32)
        return (total + lax.optimization_barrier(part.astype(jnp.bfloat16)).astype(jnp.float32), None)
    pulled, _ = lax.scan(add_block, jnp.zeros((ITEMS, DS), jnp.float32), jnp.arange(N_FEAT, dtype=jnp.int32))
    push = jnp.dot(student, gram_b, preferred_element_type=jnp.float32)
    dstudent = (push - pulled) / float(ITEMS)
    drecon = inv * (dstudent - s_full * lax.optimization_barrier(jnp.mean(dstudent * s_full, axis=-1, keepdims=True)))
    grads = jnp.stack([jax.ops.segment_sum(drecon, codes[:, level], num_segments=CODES) for level in range(LEVELS)])
    return (loss, grads)
```

```python
import jax
import jax.numpy as jnp
from jax import lax
from jax.experimental import pallas as pl
from jax.experimental.pallas import tpu as pltpu
from jax.sharding import Mesh
from jax.sharding import PartitionSpec as P

DT = 4096
DS = 512
EPS = 1e-06
F32 = jnp.float32
BF16 = jnp.bfloat16
FEAT = ("xh", "za", "zb")
ITEM = ("y", "xl", "c")
ROWS = 576
CHUNK = 512

NT = (((1,), (1,)), ((), ()))


def lanes_of(packed_ref, row, start, count):
    return jnp.concatenate([packed_ref[start + j, row : row + 1, :] for j in range(count)], axis=1)


def codes_of(packed_ref, level, start, count):
    return lanes_of(packed_ref, 16 + level, start, count).astype(jnp.int32)


def cross_kernel(where_ref, packed_ref, teacher_ref, book_ref, keep_ref, send_ref, student_ref, tnorm_ref, inv_ref, table, parts):
    item, feat, me = where_ref[0], where_ref[1], where_ref[2]
    low = item & 7
    picked = jnp.concatenate(
        [
            book_ref[0, item],
            book_ref[0, (item + 1) & 15],
            book_ref[1, 2 * low],
            book_ref[1, 2 * low + 1],
            book_ref[2].reshape(256, DS),
            book_ref[3].reshape(256, DS),
        ],
        axis=0,
    )
    table[...] = picked.astype(F32).T.astype(BF16)
    per = CHUNK // 128
    small = lax.broadcasted_iota(jnp.int32, (32, CHUNK), 0)
    large = lax.broadcasted_iota(jnp.int32, (256, CHUNK), 0)
    for n in range(2048 // CHUNK):
        first = (codes_of(packed_ref, 0, n * per, per) - 16 * item) & 255
        second = codes_of(packed_ref, 1, n * per, per) - 32 * low
        onehot = jnp.concatenate(
            [
                (small == first).astype(F32),
                (small == second).astype(F32),
                (large == codes_of(packed_ref, 2, n * per, per)).astype(F32),
                (large == codes_of(packed_ref, 3, n * per, per)).astype(F32),
            ],
            axis=0,
        ).astype(BF16)
        recon = jnp.dot(table[...], onehot, preferred_element_type=F32)
        inv = lax.rsqrt(jnp.sum(recon * recon, axis=0, keepdims=True) / DS + EPS)
        student_ref[:, n * CHUNK : (n + 1) * CHUNK] = (recon * inv).astype(BF16)
        inv_ref[:, n * CHUNK : (n + 1) * CHUNK] = inv
    squares = packed_ref[0, 0:16, :]
    for j in range(1, 16):
        squares = squares + packed_ref[j, 0:16, :]
    factor = lax.rsqrt(squares / DT + EPS)
    for j in range(16):
        column = jnp.broadcast_to(factor[j : j + 1, :], (128, 128)).T
        rows = teacher_ref[j * 128 : (j + 1) * 128, :].astype(F32)
        tnorm_ref[j * 128 : (j + 1) * 128, :] = (rows * jnp.concatenate([column, column], axis=1)).astype(BF16)
    student = student_ref[...]
    cross = jnp.dot(student, tnorm_ref[...], preferred_element_type=F32)
    mine = student_ref[pl.ds(pl.multiple_of(feat * 32, 32), 32), :]
    gram = lax.dot_general(mine, student, NT, preferred_element_type=F32)
    for b in range(4):
        to = b ^ me
        parts[to, 0:128, :] = cross[b * 128 : (b + 1) * 128, 0:128]
        parts[to, 128:256, :] = cross[b * 128 : (b + 1) * 128, 128:256]
        parts[to, 256:288, :] = gram[:, b * 128 : (b + 1) * 128]
    keep_ref[...] = parts[0:2]
    send_ref[...] = parts[2:4].astype(BF16)


def grad_kernel(where_ref, packed_ref, whole_ref, student_ref, tnorm_ref, inv_ref, keep_ref, send_ref, near_ref, other_ref, next_ref, loss_ref, cross, gram):
    item, feat, me = where_ref[0], where_ref[1], where_ref[2]
    place, zb, half = where_ref[3], where_ref[4], where_ref[5]
    for b in range(4):
        block = whole_ref[b ^ me]
        cross[b * 128 : (b + 1) * 128, 0:128] = block[0:128]
        cross[b * 128 : (b + 1) * 128, 128:256] = block[128:256]
        gram[:, b * 128 : (b + 1) * 128] = block[256:288]
    cross_f = cross[...].astype(F32)
    gram_f = gram[...].astype(F32)
    loss = jnp.sum(gram_f * gram_f, keepdims=True) - 2.0 * jnp.sum(cross_f * cross_f, keepdims=True)
    loss_ref[...] = jnp.broadcast_to(loss, (8, 128))
    gram_t = gram_f.T.astype(BF16)
    per = CHUNK // 128
    total = jnp.zeros((ROWS, DS), F32)
    large = lax.broadcasted_iota(jnp.int32, (512, CHUNK), 0)
    small = lax.broadcasted_iota(jnp.int32, (64, CHUNK), 0) + 512
    for n in range(2048 // CHUNK):
        span = slice(n * CHUNK, (n + 1) * CHUNK)
        mine = student_ref[pl.ds(pl.multiple_of(feat * 32, 32), 32), span]
        push = jnp.dot(gram_t, mine, preferred_element_type=F32)
        pull = lax.dot_general(cross[...], tnorm_ref[span, :], NT, preferred_element_type=F32)
        value = push - pull
        student = student_ref[:, span].astype(F32)
        mean = jnp.sum(value * student, axis=0, keepdims=True) / DS
        grad = ((value - student * mean) * (inv_ref[:, span] / 32768.0)).astype(BF16)

        def spot(code, level):
            low = code & 15
            return (((code >> 4) ^ place) << 5) + (((low >> 3) ^ zb) << 4) + 8 * level + (low & 7)

        first = (codes_of(packed_ref, 0, n * per, per) - 16 * item) & 255
        own = 512 + (((first >> 3) ^ zb) << 4) + (first & 7)
        first = jnp.where(first < 16, own, 560 + (zb << 3))
        second = codes_of(packed_ref, 1, n * per, per) - 32 * (item & 7)
        low = second & 15
        side = (low >> 3) ^ zb
        second = jnp.where(
            ((second >> 4) ^ half) == 0, 520 + (side << 4) + (low & 7), 544 + (side << 3) + (low & 7)
        )
        third = spot(codes_of(packed_ref, 2, n * per, per), 0)
        fourth = spot(codes_of(packed_ref, 3, n * per, per), 1)
        onehot = jnp.concatenate(
            [
                ((large == third) | (large == fourth)).astype(F32),
                ((small == first) | (small == second)).astype(F32),
            ],
            axis=0,
        ).astype(BF16)
        total = total + lax.dot_general(onehot, grad, NT, preferred_element_type=F32)
    keep_ref[...] = total[0:256].reshape(keep_ref.shape)
    send_ref[...] = total[256:512].reshape(send_ref.shape).astype(BF16)
    near_ref[...] = total[512:544].reshape(near_ref.shape)
    other_ref[...] = total[544:560].reshape(other_ref.shape).astype(BF16)
    next_ref[...] = total[560:576].reshape(next_ref.shape).astype(BF16)


def spread_kernel(where_ref, *refs):
    *pieces, out_ref = refs
    place, zb = where_ref[3], where_ref[4]
    for rank, piece in enumerate(pieces):
        for y in range(4):
            at = (rank * 4 + y) ^ place
            ay, axl, ac = at & 3, (at >> 2) & 1, at >> 3
            row0 = (ay * 4 + axl * 2 + ac) * 16
            row1 = ((ay & 1) * 4 + axl * 2 + ac) * 32 + (ay >> 1) * 16
            row2 = at * 16
            for z in range(2):
                shift = (z ^ zb) * 8
                out_ref[2, pl.ds(pl.multiple_of(row2 + shift, 8), 8), :] = piece[y, z, 0].astype(F32)
                out_ref[3, pl.ds(pl.multiple_of(row2 + shift, 8), 8), :] = piece[y, z, 1].astype(F32)
                out_ref[0, pl.ds(pl.multiple_of(row0 + shift, 8), 8), :] = piece[y, z, 2].astype(F32)
                out_ref[1, pl.ds(pl.multiple_of(row1 + shift, 8), 8), :] = piece[y, z, 3].astype(F32)


def call(kernel, outs, scratch=()):
    smem = pl.BlockSpec(memory_space=pltpu.SMEM)
    vmem = pl.BlockSpec(memory_space=pltpu.VMEM)

    def run(where, *args):
        return pl.pallas_call(
            kernel,
            out_shape=[jax.ShapeDtypeStruct(s, d) for s, d in outs],
            in_specs=[smem] + [vmem] * len(args),
            out_specs=[vmem] * len(outs),
            scratch_shapes=list(scratch),
            compiler_params=pltpu.CompilerParams(vmem_limit_bytes=48 << 20),
        )(where, *args)

    return run


def swap(array, axis, size, bit):
    return lax.ppermute(array, axis, [(j, j ^ bit) for j in range(size)])


def pieces_of(value):
    high = value.astype(BF16)
    rest = value - high.astype(F32)
    middle = rest.astype(BF16)
    low = (rest - middle.astype(F32)).astype(BF16)
    return jnp.stack([high, middle, low])


def on_device(teacher, codebooks, codes):
    y, xl, c = lax.axis_index("y"), lax.axis_index("xl"), lax.axis_index("c")
    zb = lax.axis_index("zb")
    item = y * 4 + xl * 2 + c
    feat = lax.axis_index(FEAT)
    where = jnp.stack([item, feat, c * 2 + xl, c * 8 + xl * 4 + y, zb, y >> 1]).astype(jnp.int32)

    tfull = teacher.astype(F32)
    squares = jnp.sum(tfull * tfull, axis=-1).reshape(16, 128)
    packed = jnp.concatenate([squares, codes.T.astype(F32)], axis=0)
    packed = lax.all_to_all(jnp.broadcast_to(packed[None], (16, 20, 128)), FEAT, 0, 0, tiled=True)

    keep, send, student, tnorm, inv = call(
        cross_kernel,
        [((2, 288, 128), F32), ((2, 288, 128), BF16), ((DS, 2048), BF16), ((2048, 256), BF16), ((1, 2048), F32)],
        [pltpu.VMEM((DS, ROWS), BF16), pltpu.VMEM((4, 288, 128), F32)],
    )(where, packed, teacher, codebooks.reshape(4, 16, 16, DS))

    part = keep + swap(send, "c", 2, 1).astype(F32)
    part = part[0] + swap(part[1].astype(BF16), "xl", 2, 1).astype(F32)
    own = part.astype(BF16)
    a, b, d = (swap(own, "y", 4, k) for k in (1, 2, 3))
    whole = ((own.astype(F32) + a.astype(F32)) + (b.astype(F32) + d.astype(F32))).astype(BF16)
    whole = jnp.stack([whole, swap(whole, "xl", 2, 1)])
    whole = jnp.concatenate([whole, swap(whole, "c", 2, 1)])

    keep, send, near, other, after, loss = call(
        grad_kernel,
        [
            ((2, 4, 2, 2, 8, DS), F32),
            ((2, 4, 2, 2, 8, DS), BF16),
            ((2, 2, 8, DS), F32),
            ((2, 8, DS), BF16),
            ((2, 8, DS), BF16),
            ((8, 128), F32),
        ],
        [pltpu.VMEM((DS, 256), BF16), pltpu.VMEM((32, DS), BF16)],
    )(where, packed, whole, student, tnorm, inv)

    after = lax.ppermute(after, ITEM, [(j, (j + 1) % 16) for j in range(16)])
    other = swap(other, "y", 4, 2)
    sums = keep + swap(send, "c", 2, 1).astype(F32)
    sums = sums[0] + swap(sums[1].astype(BF16), "xl", 2, 1).astype(F32)
    sent = sums[1:].astype(BF16)
    sums = sums[0]
    for k in (1, 2, 3):
        sums = sums + swap(sent[k - 1], "y", 4, k).astype(F32)
    near = near + jnp.stack([after, other], axis=1).astype(F32)
    rows = jnp.concatenate([sums, near], axis=1)

    scalar = jnp.zeros((1, 8, DS), BF16)
    loss = loss[0, 0]
    scalar = scalar.at[0, 0, 0:3].set(pieces_of(loss))
    sent = jnp.concatenate([rows[1].astype(BF16), scalar])
    got = swap(sent, "zb", 2, 1).astype(F32)
    loss = loss + jnp.sum(got[4, 0, 0:3])
    rows = rows[0] + got[0:4]
    scalar = jnp.zeros((1, 8, DS), BF16).at[0, 0, 0:3].set(pieces_of(loss))
    sent = jnp.concatenate([rows.astype(BF16), scalar])
    got = lax.all_to_all(jnp.broadcast_to(sent[None], (8, 5, 8, DS)), ("xh", "za"), 0, 0, tiled=True)
    got = jnp.sum(got.astype(F32), axis=0)
    loss = jnp.sum(got[4, 0, 0:3]) / (32768.0 * 32768.0 * DS)

    rows = got[0:4].astype(BF16)
    rows = jnp.stack([rows, swap(rows, "zb", 2, 1)])
    rows = jnp.stack([rows] + [swap(rows, "y", 4, k) for k in (1, 2, 3)])
    beside = swap(rows, "xl", 2, 1)
    far = swap(rows, "c", 2, 1)
    far_beside = swap(beside, "c", 2, 1)
    (grads,) = call(spread_kernel, [((4, 256, DS), F32)])(where, rows, beside, far, far_beside)
    return (loss, grads)


def solution(mesh):
    split = Mesh(mesh.devices.reshape(4, 2, 2, 2, 4, 2), ITEM + FEAT)
    return jax.shard_map(
        on_device,
        mesh=split,
        in_specs=(P(ITEM, FEAT), P(), P(ITEM + FEAT, None)),
        out_specs=(P(), P()),
        check_vma=False,
    )
```

```python
import jax
import jax.numpy as jnp
from jax import lax
from jax.experimental import pallas as pl
from jax.experimental.pallas import tpu as pltpu
from jax.sharding import Mesh
from jax.sharding import PartitionSpec as P

DT = 4096
DS = 512
EPS = 1e-06
F32 = jnp.float32
BF16 = jnp.bfloat16
FEAT = ("xh", "za", "zb")
ITEM = ("y", "xl", "c")
ROWS = 576
CHUNK = 512

NT = (((1,), (1,)), ((), ()))
ANY, HBM, SMEM, VMEM = pl.ANY, pltpu.HBM, pltpu.SMEM, pltpu.VMEM


def lanes_of(packed_ref, row, start, count):
    return jnp.concatenate([packed_ref[start + j, row : row + 1, :] for j in range(count)], axis=1)


def codes_of(packed_ref, level, start, count):
    return lanes_of(packed_ref, 16 + level, start, count).astype(jnp.int32)


def pack_kernel(teacher_hbm, codes_hbm, teacher_ref, packed_ref, codes_ref, gathered, sems):
    first = pltpu.make_async_copy(codes_hbm, codes_ref, sems.at[4])
    first.start()
    copies = []
    for n in range(4):
        rows = pl.ds(n * 512, 512)
        copies.append(pltpu.make_async_copy(teacher_hbm.at[rows], teacher_ref.at[rows], sems.at[n]))
        copies[-1].start()
    first.wait()
    gathered[16:20, :] = codes_ref[...].astype(F32)
    gathered[20:24, :] = jnp.zeros((4, 128), F32)
    ones = jnp.ones((8, 256), BF16)
    for n in range(4):
        copies[n].wait()
        rows = teacher_ref[n * 512 : (n + 1) * 512, :].astype(F32)
        squares = rows * rows
        upper = squares.astype(BF16)
        lower = (squares - upper.astype(F32)).astype(BF16)
        sums = lax.dot_general(ones, upper, NT, preferred_element_type=F32)
        sums = sums + lax.dot_general(ones, lower, NT, preferred_element_type=F32)
        for j in range(4):
            gathered[4 * n + j : 4 * n + j + 1, :] = sums[0:1, j * 128 : (j + 1) * 128]
    packed_ref[...] = gathered[...].astype(BF16)


def table_kernel(where_ref, book_ref, table_ref):
    item = where_ref[0]
    low = item & 7
    picked = jnp.concatenate(
        [
            book_ref[0, item],
            book_ref[0, (item + 1) & 15],
            book_ref[1, 2 * low],
            book_ref[1, 2 * low + 1],
            book_ref[2].reshape(256, DS),
            book_ref[3].reshape(256, DS),
        ],
        axis=0,
    )
    table_ref[...] = picked.astype(F32).T.astype(BF16)


def cross_kernel(where_ref, packed_ref, teacher_ref, table_ref, keep_ref, send_ref, student_ref, tnorm_ref, inv_ref, packed):
    packed[...] = packed_ref[...].astype(F32)
    item, feat, me = where_ref[0], where_ref[1], where_ref[2]
    low = item & 7
    table = table_ref[...]
    per = CHUNK // 128
    small = lax.broadcasted_iota(jnp.int32, (32, CHUNK), 0)
    large = lax.broadcasted_iota(jnp.int32, (256, CHUNK), 0)
    for n in range(2048 // CHUNK):
        first = (codes_of(packed, 0, n * per, per) - 16 * item) & 255
        second = codes_of(packed, 1, n * per, per) - 32 * low
        onehot = jnp.concatenate(
            [
                (small == first).astype(F32),
                (small == second).astype(F32),
                (large == codes_of(packed, 2, n * per, per)).astype(F32),
                (large == codes_of(packed, 3, n * per, per)).astype(F32),
            ],
            axis=0,
        ).astype(BF16)
        recon = jnp.dot(table, onehot, preferred_element_type=F32)
        inv = lax.rsqrt(jnp.sum(recon * recon, axis=0, keepdims=True) / DS + EPS)
        student_ref[:, n * CHUNK : (n + 1) * CHUNK] = (recon * inv).astype(BF16)
        inv_ref[:, n * CHUNK : (n + 1) * CHUNK] = inv
    squares = packed[0, 0:16, :]
    for j in range(1, 16):
        squares = squares + packed[j, 0:16, :]
    factor = lax.rsqrt(squares / DT + EPS)
    for j in range(16):
        column = jnp.broadcast_to(factor[j : j + 1, :], (128, 128)).T
        rows = teacher_ref[j * 128 : (j + 1) * 128, :].astype(F32)
        tnorm_ref[j * 128 : (j + 1) * 128, :] = (rows * jnp.concatenate([column, column], axis=1)).astype(BF16)
    student = student_ref[...]
    cross = jnp.dot(student, tnorm_ref[...], preferred_element_type=F32)
    mine = student_ref[pl.ds(pl.multiple_of(feat * 32, 32), 32), :]
    gram = lax.dot_general(mine, student, NT, preferred_element_type=F32)
    for b in range(4):
        to = b ^ me

        def store(ref, at):
            ref[at, 0:128, :] = cross[b * 128 : (b + 1) * 128, 0:128]
            ref[at, 128:256, :] = cross[b * 128 : (b + 1) * 128, 128:256]
            ref[at, 256:288, :] = gram[:, b * 128 : (b + 1) * 128]

        @pl.when(to < 2)
        def _():
            store(keep_ref, to)

        @pl.when(to >= 2)
        def _():
            store(send_ref, to - 2)


def grad_kernel(where_ref, packed_ref, whole_ref, student_ref, tnorm_ref, inv_ref, keep_ref, send_ref, near_ref, other_ref, loss_ref, cross, gram, packed):
    packed[...] = packed_ref[...].astype(F32)
    item, feat, me = where_ref[0], where_ref[1], where_ref[2]
    place, zb, half = where_ref[3], where_ref[4], where_ref[5]
    for b in range(4):
        block = whole_ref[b ^ me]
        cross[b * 128 : (b + 1) * 128, 0:128] = block[0:128]
        cross[b * 128 : (b + 1) * 128, 128:256] = block[128:256]
        gram[:, b * 128 : (b + 1) * 128] = block[256:288]
    cross_f = cross[...].astype(F32)
    gram_f = gram[...].astype(F32)
    loss = jnp.sum(gram_f * gram_f, keepdims=True) - 2.0 * jnp.sum(cross_f * cross_f, keepdims=True)
    high = loss.astype(BF16).astype(F32)
    middle = (loss - high).astype(BF16).astype(F32)
    rest = (loss - high - middle).astype(BF16).astype(F32)
    row = lax.broadcasted_iota(jnp.int32, (8, DS), 0)
    lane = lax.broadcasted_iota(jnp.int32, (8, DS), 1)
    parts = jnp.where(row == 0, high, jnp.where(row == 1, middle, jnp.where(row == 2, rest, 0.0)))
    loss_ref[...] = jnp.where(lane == feat, parts, 0.0)
    gram_t = gram_f.T.astype(BF16)
    per = CHUNK // 128
    total = jnp.zeros((ROWS, DS), F32)
    large = lax.broadcasted_iota(jnp.int32, (512, CHUNK), 0)
    small = lax.broadcasted_iota(jnp.int32, (64, CHUNK), 0) + 512
    for n in range(2048 // CHUNK):
        span = slice(n * CHUNK, (n + 1) * CHUNK)
        mine = student_ref[pl.ds(pl.multiple_of(feat * 32, 32), 32), span]
        push = jnp.dot(gram_t, mine, preferred_element_type=F32)
        pull = lax.dot_general(cross[...], tnorm_ref[span, :], NT, preferred_element_type=F32)
        value = push - pull
        student = student_ref[:, span].astype(F32)
        mean = jnp.sum(value * student, axis=0, keepdims=True) / DS
        grad = ((value - student * mean) * (inv_ref[:, span] / 32768.0)).astype(BF16)

        def spot(code, level):
            low = code & 15
            return (((code >> 4) ^ place) << 5) + (((low >> 3) ^ zb) << 4) + 8 * level + (low & 7)

        first = (codes_of(packed, 0, n * per, per) - 16 * item) & 255
        own = 512 + (((first >> 3) ^ zb) << 4) + (first & 7)
        first = jnp.where(first < 16, own, 560)
        second = codes_of(packed, 1, n * per, per) - 32 * (item & 7)
        low = second & 15
        side = (low >> 3) ^ zb
        second = jnp.where(
            ((second >> 4) ^ half) == 0, 520 + (side << 4) + (low & 7), 544 + (side << 3) + (low & 7)
        )
        third = spot(codes_of(packed, 2, n * per, per), 0)
        fourth = spot(codes_of(packed, 3, n * per, per), 1)
        onehot = jnp.concatenate(
            [
                ((large == third) | (large == fourth)).astype(F32),
                ((small == first) | (small == second)).astype(F32),
            ],
            axis=0,
        ).astype(BF16)
        total = total + lax.dot_general(onehot, grad, NT, preferred_element_type=F32)
    keep_ref[...] = total[0:256].reshape(keep_ref.shape)
    send_ref[0:32] = total[256:512].reshape(32, 8, DS)
    send_ref[32] = total[560:568]
    near_ref[...] = total[512:544].reshape(near_ref.shape)
    other_ref[...] = total[544:560].reshape(other_ref.shape).astype(BF16)


def spread_half(c, where_ref, piece_ref, out_hbm, rows, sems):
    place, zb = where_ref[3], where_ref[4]
    kept = c ^ (place >> 3)
    for x in range(2):
        for y in range(4):
            at = (x * 4 + y) ^ (place & 7)
            ay, axl = at & 3, at >> 2
            row0 = (ay * 2 + axl) * 16
            row1 = ((ay & 1) * 2 + axl) * 32 + (ay >> 1) * 16
            row2 = at * 16
            for z in range(2):
                shift = (z ^ zb) * 8
                for k, (level, row) in enumerate(((2, row2), (3, row2), (0, row0), (1, row1))):
                    rows[level, pl.ds(pl.multiple_of(row + shift, 8), 8), :] = piece_ref[x * 4 + y, z, k].astype(F32)
    copies = []

    def copy(level, start, count, to):
        target = out_hbm.at[level, pl.ds(pl.multiple_of(to, 16), count)]
        copies.append(pltpu.make_async_copy(rows.at[level, pl.ds(start, count)], target, sems.at[len(copies)]))
        copies[-1].start()

    copy(2, 0, 128, kept * 128)
    copy(3, 0, 128, kept * 128)
    for j in range(8):
        copy(0, j * 16, 16, (j * 2 + (kept ^ (j & 1) ^ ((j >> 1) & 1))) * 16)
    for j in range(4):
        copy(1, j * 32, 32, (j * 2 + (kept ^ (j & 1) ^ (j >> 1))) * 32)
    for one in copies:
        one.wait()


def near_kernel(where_ref, piece_ref, parts_ref, out_hbm, loss_ref, rows, sems):
    loss_ref[...] = jnp.sum(parts_ref[...], keepdims=True) / (32768.0 * 32768.0 * DS)
    spread_half(0, where_ref, piece_ref, out_hbm, rows, sems)


def far_kernel(where_ref, piece_ref, begun_hbm, out_hbm, rows, sems):
    spread_half(1, where_ref, piece_ref, out_hbm, rows, sems)


def call(kernel, ins, outs, scratch=(), aliases=None):
    return pl.pallas_call(
        kernel,
        out_shape=[jax.ShapeDtypeStruct(shape, kind) for shape, kind, _ in outs],
        in_specs=[pl.BlockSpec(memory_space=space) for space in ins],
        out_specs=[pl.BlockSpec(memory_space=space) for _, _, space in outs],
        scratch_shapes=list(scratch),
        input_output_aliases=aliases or {},
        compiler_params=pltpu.CompilerParams(vmem_limit_bytes=48 << 20),
    )


def swap(array, axis, size, bit):
    return lax.ppermute(array, axis, [(j, j ^ bit) for j in range(size)])


def in_hbm(array):
    return pltpu.with_memory_space_constraint(array, pltpu.HBM)


def across_x(array):
    return swap(array, ("xl", "c"), 4, 3)


def across_y(array, bits):
    return swap(array, ("y", "c"), 8, 2 * bits + (bits & 1))


def on_device(teacher, codebooks, codes):
    y, xl, c = lax.axis_index("y"), lax.axis_index("xl"), lax.axis_index("c")
    zb = lax.axis_index("zb")
    item = y * 4 + xl * 2 + c
    feat = lax.axis_index(FEAT)
    kept = c ^ xl ^ (y & 1)
    where = jnp.stack([item, feat, kept * 2 + xl, kept * 8 + xl * 4 + y, zb, y >> 1]).astype(jnp.int32)

    teacher, packed = call(
        pack_kernel,
        [HBM, HBM],
        [((2048, 256), BF16, VMEM), ((24, 128), BF16, VMEM)],
        [pltpu.VMEM((4, 128), jnp.int32), pltpu.VMEM((24, 128), F32), pltpu.SemaphoreType.DMA((5,))],
    )(in_hbm(teacher), in_hbm(codes.T))
    packed = lax.all_to_all(jnp.broadcast_to(packed[None], (16, 24, 128)), FEAT, 0, 0, tiled=True)
    (table,) = call(table_kernel, [SMEM, VMEM], [((DS, ROWS), BF16, VMEM)])(where, codebooks.reshape(4, 16, 16, DS))

    keep, send, student, tnorm, inv = call(
        cross_kernel,
        [SMEM, VMEM, VMEM, VMEM],
        [
            ((2, 288, 128), F32, VMEM),
            ((2, 288, 128), F32, VMEM),
            ((DS, 2048), BF16, VMEM),
            ((2048, 256), BF16, VMEM),
            ((1, 2048), F32, VMEM),
        ],
        [pltpu.VMEM((16, 24, 128), F32)],
    )(where, packed, teacher, table)

    part = keep + swap(send, "c", 2, 1)
    part = part[0] + across_x(part[1].astype(BF16)).astype(F32)
    own = part.astype(BF16)
    a, b, d = (across_y(own, k) for k in (1, 2, 3))
    whole = ((own.astype(F32) + a.astype(F32)) + (b.astype(F32) + d.astype(F32))).astype(BF16)
    whole = jnp.stack([whole, across_x(whole)])
    whole = jnp.concatenate([whole, swap(whole, "c", 2, 1)])

    keep, send, near, other, loss = call(
        grad_kernel,
        [SMEM] + [VMEM] * 5,
        [
            ((32, 8, DS), F32, VMEM),
            ((33, 8, DS), F32, VMEM),
            ((2, 2, 8, DS), F32, VMEM),
            ((2, 8, DS), BF16, VMEM),
            ((8, DS), F32, VMEM),
        ],
        [pltpu.VMEM((DS, 256), BF16), pltpu.VMEM((32, DS), BF16), pltpu.VMEM((16, 24, 128), F32)],
    )(where, packed, whole, student, tnorm, inv)

    got = swap(send, "c", 2, 1)
    sums = keep + got[:32]
    none = jnp.zeros((), BF16)
    extra = jnp.where(c == 1, got[32], 0.0)
    ahead = jnp.where((c == 1) & (xl == 0), send[32:], jnp.where((c == 0) & (xl == 1), got[32:], 0.0))
    got = across_x(jnp.concatenate([sums[16:].astype(BF16), ahead.astype(BF16)]))
    sums = sums[:16] + got[:16].astype(F32)
    extra = extra + jnp.where((c == 0) & (xl == 1), got[16].astype(F32), 0.0)
    ahead = jnp.where((c == 1) & (xl == 0), got[16:], none)
    odd = (y & 1) == 1
    one = across_y(jnp.concatenate([sums[4:8].astype(BF16), jnp.where(odd, none, ahead)]), 1)
    two = across_y(jnp.concatenate([sums[8:12].astype(BF16), other]), 2)
    three = across_y(jnp.concatenate([sums[12:16].astype(BF16), jnp.where(odd, ahead, none)]), 3)
    sums = sums[0:4] + one[:4].astype(F32) + two[:4].astype(F32) + three[:4].astype(F32)
    extra = extra + one[4].astype(F32) + three[4].astype(F32)

    def rows_of(z):
        zero = near[z, 0] + jnp.where(zb == z, extra, 0.0)
        first = near[z, 1] + two[4 + z].astype(F32)
        return jnp.concatenate([sums[2 * z : 2 * z + 2], zero[None], first[None], loss[None]])

    rows = rows_of(0) + swap(rows_of(1).astype(BF16), "zb", 2, 1).astype(F32)
    sent = jnp.broadcast_to(rows.astype(BF16)[None], (8, 5, 8, DS))
    got = lax.all_to_all(sent, ("xh", "za"), 0, 0, tiled=True)
    rows = jnp.sum(got.astype(F32), axis=0)
    loss = rows[4]
    rows = rows[:4].astype(BF16)

    rows = jnp.stack([rows, swap(rows, "zb", 2, 1)])
    rows = jnp.stack([rows] + [across_y(rows, k) for k in (1, 2, 3)])
    rows = jnp.concatenate([rows, across_x(rows[:2]), swap(rows[2:], ("xl", "c", "xh"), 8, 7)])
    far = swap(rows, "c", 2, 1)
    rows_and_sems = [pltpu.VMEM((4, 128, DS), F32), pltpu.SemaphoreType.DMA((14,))]
    grads, loss = call(
        near_kernel, [SMEM, VMEM, VMEM], [((4, 256, DS), F32, ANY), ((1, 1), F32, VMEM)], rows_and_sems
    )(where, rows, loss)
    (grads,) = call(far_kernel, [SMEM, VMEM, ANY], [((4, 256, DS), F32, ANY)], rows_and_sems, {2: 0})(where, far, grads)
    return (loss.reshape(()), grads)


def solution(mesh):
    split = Mesh(mesh.devices.reshape(4, 2, 2, 2, 4, 2), ITEM + FEAT)
    return jax.shard_map(
        on_device,
        mesh=split,
        in_specs=(P(ITEM, FEAT), P(), P(ITEM + FEAT, None)),
        out_specs=(P(), P()),
        check_vma=False,
    )
```

```python
import jax
import jax.numpy as jnp
from jax import lax
from jax.experimental import pallas as pl
from jax.experimental.pallas import tpu as pltpu
from jax.sharding import Mesh
from jax.sharding import PartitionSpec as P

DT = 4096
DS = 512
EPS = 1e-06
F32 = jnp.float32
BF16 = jnp.bfloat16
FEAT = ("xh", "za", "zb")
ITEM = ("y", "xl", "c")
ROWS = 576
CHUNK = 512

NT = (((1,), (1,)), ((), ()))
ANY, HBM, SMEM, VMEM = pl.ANY, pltpu.HBM, pltpu.SMEM, pltpu.VMEM


def lanes_of(packed_ref, row, start, count):
    return jnp.concatenate([packed_ref[start + j, row : row + 1, :] for j in range(count)], axis=1)


def codes_of(packed_ref, level, start, count):
    return lanes_of(packed_ref, 16 + level, start, count).astype(jnp.int32)


def pack_kernel(teacher_hbm, codes_hbm, teacher_ref, packed_ref, codes_ref, gathered, sems):
    first = pltpu.make_async_copy(codes_hbm, codes_ref, sems.at[4])
    first.start()
    copies = []
    for n in range(4):
        rows = pl.ds(n * 512, 512)
        copies.append(pltpu.make_async_copy(teacher_hbm.at[rows], teacher_ref.at[rows], sems.at[n]))
        copies[-1].start()
    first.wait()
    gathered[16:20, :] = codes_ref[...].astype(F32)
    gathered[20:24, :] = jnp.zeros((4, 128), F32)
    ones = jnp.ones((8, 256), BF16)
    for n in range(4):
        copies[n].wait()
        rows = teacher_ref[n * 512 : (n + 1) * 512, :].astype(F32)
        squares = rows * rows
        upper = squares.astype(BF16)
        lower = (squares - upper.astype(F32)).astype(BF16)
        sums = lax.dot_general(ones, upper, NT, preferred_element_type=F32)
        sums = sums + lax.dot_general(ones, lower, NT, preferred_element_type=F32)
        for j in range(4):
            gathered[4 * n + j : 4 * n + j + 1, :] = sums[0:1, j * 128 : (j + 1) * 128]
    packed_ref[...] = gathered[...].astype(BF16)


def table_kernel(where_ref, book_ref, table_ref):
    item = where_ref[0]
    low = item & 7
    picked = jnp.concatenate(
        [
            book_ref[0, item],
            book_ref[0, (item + 1) & 15],
            book_ref[1, 2 * low],
            book_ref[1, 2 * low + 1],
            book_ref[2].reshape(256, DS),
            book_ref[3].reshape(256, DS),
        ],
        axis=0,
    )
    table_ref[...] = picked.astype(F32).T.astype(BF16)


def cross_kernel(where_ref, packed_ref, teacher_ref, table_ref, keep_ref, send_ref, student_ref, tnorm_ref, inv_ref, packed):
    packed[...] = packed_ref[...].astype(F32)
    item, feat, me = where_ref[0], where_ref[1], where_ref[2]
    low = item & 7
    table = table_ref[...]
    per = CHUNK // 128
    small = lax.broadcasted_iota(jnp.int32, (32, CHUNK), 0)
    large = lax.broadcasted_iota(jnp.int32, (256, CHUNK), 0)
    for n in range(2048 // CHUNK):
        first = (codes_of(packed, 0, n * per, per) - 16 * item) & 255
        second = codes_of(packed, 1, n * per, per) - 32 * low
        onehot = jnp.concatenate(
            [
                (small == first).astype(F32),
                (small == second).astype(F32),
                (large == codes_of(packed, 2, n * per, per)).astype(F32),
                (large == codes_of(packed, 3, n * per, per)).astype(F32),
            ],
            axis=0,
        ).astype(BF16)
        recon = jnp.dot(table, onehot, preferred_element_type=F32)
        inv = lax.rsqrt(jnp.sum(recon * recon, axis=0, keepdims=True) / DS + EPS)
        student_ref[:, n * CHUNK : (n + 1) * CHUNK] = (recon * inv).astype(BF16)
        inv_ref[:, n * CHUNK : (n + 1) * CHUNK] = inv
    squares = packed[0, 0:16, :]
    for j in range(1, 16):
        squares = squares + packed[j, 0:16, :]
    factor = lax.rsqrt(squares / DT + EPS)
    for j in range(16):
        column = jnp.broadcast_to(factor[j : j + 1, :], (128, 128)).T
        rows = teacher_ref[j * 128 : (j + 1) * 128, :].astype(F32)
        tnorm_ref[j * 128 : (j + 1) * 128, :] = (rows * jnp.concatenate([column, column], axis=1)).astype(BF16)
    student = student_ref[...]
    cross = jnp.dot(student, tnorm_ref[...], preferred_element_type=F32)
    mine = student_ref[pl.ds(pl.multiple_of(feat * 32, 32), 32), :]
    gram = lax.dot_general(mine, student, NT, preferred_element_type=F32)
    for b in range(4):
        to = b ^ me

        def store(ref, at):
            ref[at, 0:128, :] = cross[b * 128 : (b + 1) * 128, 0:128]
            ref[at, 128:256, :] = cross[b * 128 : (b + 1) * 128, 128:256]
            ref[at, 256:288, :] = gram[:, b * 128 : (b + 1) * 128]

        @pl.when(to < 2)
        def _():
            store(keep_ref, to)

        @pl.when(to >= 2)
        def _():
            store(send_ref, to - 2)


def grad_kernel(where_ref, packed_ref, whole_ref, student_ref, tnorm_ref, inv_ref, keep_ref, send_ref, near_ref, other_ref, loss_ref, cross, gram, packed, grads, onehots):
    packed[...] = packed_ref[...].astype(F32)
    item, feat, me = where_ref[0], where_ref[1], where_ref[2]
    place, zb, half = where_ref[3], where_ref[4], where_ref[5]
    for b in range(4):
        block = whole_ref[b ^ me]
        cross[b * 128 : (b + 1) * 128, 0:128] = block[0:128]
        cross[b * 128 : (b + 1) * 128, 128:256] = block[128:256]
        gram[:, b * 128 : (b + 1) * 128] = block[256:288]
    cross_f = cross[...].astype(F32)
    gram_f = gram[...].astype(F32)
    loss = jnp.sum(gram_f * gram_f, keepdims=True) - 2.0 * jnp.sum(cross_f * cross_f, keepdims=True)
    high = loss.astype(BF16).astype(F32)
    middle = (loss - high).astype(BF16).astype(F32)
    rest = (loss - high - middle).astype(BF16).astype(F32)
    row = lax.broadcasted_iota(jnp.int32, (8, DS), 0)
    lane = lax.broadcasted_iota(jnp.int32, (8, DS), 1)
    parts = jnp.where(row == 0, high, jnp.where(row == 1, middle, jnp.where(row == 2, rest, 0.0)))
    loss_ref[...] = jnp.where(lane == feat, parts, 0.0)
    gram_t = gram_f.T.astype(BF16)
    per = CHUNK // 128
    large = lax.broadcasted_iota(jnp.int32, (512, CHUNK), 0)
    small = lax.broadcasted_iota(jnp.int32, (64, CHUNK), 0) + 512
    for n in range(2048 // CHUNK):
        span = slice(n * CHUNK, (n + 1) * CHUNK)
        mine = student_ref[pl.ds(pl.multiple_of(feat * 32, 32), 32), span]
        push = jnp.dot(gram_t, mine, preferred_element_type=F32)
        pull = lax.dot_general(cross[...], tnorm_ref[span, :], NT, preferred_element_type=F32)
        value = push - pull
        student = student_ref[:, span].astype(F32)
        mean = jnp.sum(value * student, axis=0, keepdims=True) / DS
        grads[:, span] = ((value - student * mean) * (inv_ref[:, span] / 32768.0)).astype(BF16)

        def spot(code, level):
            low = code & 15
            return (((code >> 4) ^ place) << 5) + (((low >> 3) ^ zb) << 4) + 8 * level + (low & 7)

        first = (codes_of(packed, 0, n * per, per) - 16 * item) & 255
        own = 512 + (((first >> 3) ^ zb) << 4) + (first & 7)
        first = jnp.where(first < 16, own, 560)
        second = codes_of(packed, 1, n * per, per) - 32 * (item & 7)
        low = second & 15
        side = (low >> 3) ^ zb
        second = jnp.where(
            ((second >> 4) ^ half) == 0, 520 + (side << 4) + (low & 7), 544 + (side << 3) + (low & 7)
        )
        third = spot(codes_of(packed, 2, n * per, per), 0)
        fourth = spot(codes_of(packed, 3, n * per, per), 1)
        onehots[0:512, span] = ((large == third) | (large == fourth)).astype(F32).astype(BF16)
        onehots[512:576, span] = ((small == first) | (small == second)).astype(F32).astype(BF16)
    total = lax.dot_general(onehots[...], grads[...], NT, preferred_element_type=F32)
    keep_ref[...] = total[0:256].reshape(keep_ref.shape)
    send_ref[0:32] = total[256:512].reshape(32, 8, DS)
    send_ref[32] = total[560:568]
    near_ref[...] = total[512:544].reshape(near_ref.shape)
    other_ref[...] = total[544:560].reshape(other_ref.shape).astype(BF16)


def spread(c, x, where_ref, piece_ref, out_hbm, rows, sems):
    place, zb = where_ref[3], where_ref[4]
    base = (c * 8 + x * 4) ^ (place & 12)
    kept, axl = base >> 3, (base >> 2) & 1
    copies = []

    def copy(level, start, count, to):
        target = out_hbm.at[level, pl.ds(pl.multiple_of(to, 16), count)]
        copies.append(pltpu.make_async_copy(rows.at[level, pl.ds(start, count)], target, sems.at[len(copies)]))
        copies[-1].start()

    for k, level in enumerate((2, 3, 0, 1)):
        for y in range(4):
            ay = y ^ (place & 3)
            row = (ay & 1) * 32 + (ay >> 1) * 16 if level == 1 else ay * 16
            for z in range(2):
                at = pl.multiple_of(row + (z ^ zb) * 8, 8)
                rows[level, pl.ds(at, 8), :] = piece_ref[y, z, k].astype(F32)
        if level == 0:
            for j in range(4):
                copy(0, j * 16, 16, (j * 4 + axl * 2 + (kept ^ axl ^ (j & 1))) * 16)
        elif level == 1:
            for j in range(2):
                copy(1, j * 32, 32, (j * 4 + axl * 2 + (kept ^ axl ^ j)) * 32)
        else:
            copy(level, 0, 64, base * 16)
    for one in copies:
        one.wait()


def first_kernel(where_ref, piece_ref, parts_ref, out_hbm, loss_ref, rows, sems):
    loss_ref[...] = jnp.sum(parts_ref[...], keepdims=True) / (32768.0 * 32768.0 * DS)
    spread(0, 0, where_ref, piece_ref, out_hbm, rows, sems)


def next_kernel(c, x):
    def kernel(where_ref, piece_ref, begun_hbm, out_hbm, *refs):
        *token, rows, sems = refs
        if token:
            token[0][...] = jnp.zeros((8, DS), BF16)
        spread(c, x, where_ref, piece_ref, out_hbm, rows, sems)

    return kernel


def call(kernel, ins, outs, scratch=(), aliases=None):
    return pl.pallas_call(
        kernel,
        out_shape=[jax.ShapeDtypeStruct(shape, kind) for shape, kind, _ in outs],
        in_specs=[pl.BlockSpec(memory_space=space) for space in ins],
        out_specs=[pl.BlockSpec(memory_space=space) for _, _, space in outs],
        scratch_shapes=list(scratch),
        input_output_aliases=aliases or {},
        compiler_params=pltpu.CompilerParams(vmem_limit_bytes=48 << 20),
    )


def swap(array, axis, size, bit):
    return lax.ppermute(array, axis, [(j, j ^ bit) for j in range(size)])


def in_hbm(array):
    return pltpu.with_memory_space_constraint(array, pltpu.HBM)


def across_x(array):
    return swap(array, ("xl", "c"), 4, 3)


def across_y(array, bits):
    return swap(array, ("y", "c"), 8, 2 * bits + (bits & 1))


def on_device(teacher, codebooks, codes):
    y, xl, c = lax.axis_index("y"), lax.axis_index("xl"), lax.axis_index("c")
    zb = lax.axis_index("zb")
    item = y * 4 + xl * 2 + c
    feat = lax.axis_index(FEAT)
    kept = c ^ xl ^ (y & 1)
    where = jnp.stack([item, feat, kept * 2 + xl, kept * 8 + xl * 4 + y, zb, y >> 1]).astype(jnp.int32)

    teacher, packed = call(
        pack_kernel,
        [HBM, HBM],
        [((2048, 256), BF16, VMEM), ((24, 128), BF16, VMEM)],
        [pltpu.VMEM((4, 128), jnp.int32), pltpu.VMEM((24, 128), F32), pltpu.SemaphoreType.DMA((5,))],
    )(in_hbm(teacher), in_hbm(codes.T))
    packed = lax.all_to_all(jnp.broadcast_to(packed[None], (16, 24, 128)), FEAT, 0, 0, tiled=True)
    (table,) = call(table_kernel, [SMEM, VMEM], [((DS, ROWS), BF16, VMEM)])(where, codebooks.reshape(4, 16, 16, DS))

    keep, send, student, tnorm, inv = call(
        cross_kernel,
        [SMEM, VMEM, VMEM, VMEM],
        [
            ((2, 288, 128), F32, VMEM),
            ((2, 288, 128), F32, VMEM),
            ((DS, 2048), BF16, VMEM),
            ((2048, 256), BF16, VMEM),
            ((1, 2048), F32, VMEM),
        ],
        [pltpu.VMEM((16, 24, 128), F32)],
    )(where, packed, teacher, table)

    part = keep + swap(send, "c", 2, 1)
    part = part[0] + across_x(part[1].astype(BF16)).astype(F32)
    own = part.astype(BF16)
    a, b, d = (across_y(own, k) for k in (1, 2, 3))
    whole = ((own.astype(F32) + a.astype(F32)) + (b.astype(F32) + d.astype(F32))).astype(BF16)
    whole = jnp.stack([whole, across_x(whole)])
    whole = jnp.concatenate([whole, swap(whole, "c", 2, 1)])

    keep, send, near, other, loss = call(
        grad_kernel,
        [SMEM] + [VMEM] * 5,
        [
            ((32, 8, DS), F32, VMEM),
            ((33, 8, DS), F32, VMEM),
            ((2, 2, 8, DS), F32, VMEM),
            ((2, 8, DS), BF16, VMEM),
            ((8, DS), F32, VMEM),
        ],
        [
            pltpu.VMEM((DS, 256), BF16),
            pltpu.VMEM((32, DS), BF16),
            pltpu.VMEM((16, 24, 128), F32),
            pltpu.VMEM((DS, 2048), BF16),
            pltpu.VMEM((ROWS, 2048), BF16),
        ],
    )(where, packed, whole, student, tnorm, inv)

    got = swap(send, "c", 2, 1)
    sums = keep + got[:32]
    none = jnp.zeros((), BF16)
    extra = jnp.where(c == 1, got[32], 0.0)
    ahead = jnp.where((c == 1) & (xl == 0), send[32:], jnp.where((c == 0) & (xl == 1), got[32:], 0.0))
    got = across_x(jnp.concatenate([sums[16:].astype(BF16), ahead.astype(BF16)]))
    sums = sums[:16] + got[:16].astype(F32)
    extra = extra + jnp.where((c == 0) & (xl == 1), got[16].astype(F32), 0.0)
    ahead = jnp.where((c == 1) & (xl == 0), got[16:], none)
    odd = (y & 1) == 1
    one = across_y(jnp.concatenate([sums[4:8].astype(BF16), jnp.where(odd, none, ahead)]), 1)
    two = across_y(jnp.concatenate([sums[8:12].astype(BF16), other]), 2)
    three = across_y(jnp.concatenate([sums[12:16].astype(BF16), jnp.where(odd, ahead, none)]), 3)
    sums = sums[0:4] + one[:4].astype(F32) + two[:4].astype(F32) + three[:4].astype(F32)
    extra = extra + one[4].astype(F32) + three[4].astype(F32)

    def rows_of(z):
        zero = near[z, 0] + jnp.where(zb == z, extra, 0.0)
        first = near[z, 1] + two[4 + z].astype(F32)
        return jnp.concatenate([sums[2 * z : 2 * z + 2], zero[None], first[None], loss[None]])

    rows = rows_of(0) + swap(rows_of(1).astype(BF16), "zb", 2, 1).astype(F32)
    own = (rows + swap(rows, "xh", 2, 1)).astype(BF16)
    a, b, d = (swap(own, "za", 4, k).astype(F32) for k in (1, 2, 3))
    rows = (own.astype(F32) + a) + (b + d)
    loss = rows[4]
    rows = rows[:4].astype(BF16)

    rows = jnp.stack([rows, swap(rows, "zb", 2, 1)])
    rows = jnp.stack([rows] + [across_y(rows, k) for k in (1, 2, 3)])
    parts = across_x(rows[:2]), swap(rows[2:], ("xl", "c", "xh"), 8, 7)
    far = swap(rows, "c", 2, 1)
    rows_and_sems = [pltpu.VMEM((4, 64, DS), F32), pltpu.SemaphoreType.DMA((8,))]
    out = ((4, 256, DS), F32, ANY)
    outs = [out, ((8, DS), BF16, VMEM)]
    grads, loss = call(first_kernel, [SMEM, VMEM, VMEM], [out, ((1, 1), F32, VMEM)], rows_and_sems)(where, rows, loss)
    grads, token = call(next_kernel(1, 0), [SMEM, VMEM, ANY], outs, rows_and_sems, {2: 0})(where, far, grads)
    beside = jnp.concatenate([part + token for part in parts])
    far_beside = swap(beside, "c", 2, 1)
    for c, piece in ((0, beside), (1, far_beside)):
        (grads,) = call(next_kernel(c, 1), [SMEM, VMEM, ANY], [out], rows_and_sems, {2: 0})(where, piece, grads)
    return (loss.reshape(()), grads)


def solution(mesh):
    split = Mesh(mesh.devices.reshape(4, 2, 2, 2, 4, 2), ITEM + FEAT)
    return jax.shard_map(
        on_device,
        mesh=split,
        in_specs=(P(ITEM, FEAT), P(), P(ITEM + FEAT, None)),
        out_specs=(P(), P()),
        check_vma=False,
    )
```

```python
import jax
import jax.numpy as jnp
from jax import lax
from jax.experimental import pallas as pl
from jax.experimental.pallas import tpu as pltpu
from jax.sharding import Mesh
from jax.sharding import PartitionSpec as P

DT = 4096
DS = 512
EPS = 1e-06
F32 = jnp.float32
BF16 = jnp.bfloat16
FEAT = ("xh", "za", "zb")
ITEM = ("y", "xl", "c")
ROWS = 576
CHUNK = 512

NT = (((1,), (1,)), ((), ()))
ANY, HBM, SMEM, VMEM = pl.ANY, pltpu.HBM, pltpu.SMEM, pltpu.VMEM


def lanes_of(packed_ref, row, start, count):
    return jnp.concatenate([packed_ref[start + j, row : row + 1, :] for j in range(count)], axis=1)


def codes_of(packed_ref, level, start, count):
    return lanes_of(packed_ref, 16 + level, start, count).astype(jnp.int32)


def pack_kernel(teacher_hbm, codes_hbm, teacher_ref, packed_ref, codes_ref, gathered, sems):
    first = pltpu.make_async_copy(codes_hbm, codes_ref, sems.at[4])
    first.start()
    copies = []
    for n in range(4):
        rows = pl.ds(n * 512, 512)
        copies.append(pltpu.make_async_copy(teacher_hbm.at[rows], teacher_ref.at[rows], sems.at[n]))
        copies[-1].start()
    first.wait()
    gathered[16:20, :] = codes_ref[...].astype(F32)
    gathered[20:24, :] = jnp.zeros((4, 128), F32)
    ones = jnp.ones((8, 256), BF16)
    for n in range(4):
        copies[n].wait()
        rows = teacher_ref[n * 512 : (n + 1) * 512, :].astype(F32)
        squares = rows * rows
        upper = squares.astype(BF16)
        lower = (squares - upper.astype(F32)).astype(BF16)
        sums = lax.dot_general(ones, upper, NT, preferred_element_type=F32)
        sums = sums + lax.dot_general(ones, lower, NT, preferred_element_type=F32)
        for j in range(4):
            gathered[4 * n + j : 4 * n + j + 1, :] = sums[0:1, j * 128 : (j + 1) * 128]
    packed_ref[...] = gathered[...].astype(BF16)


def table_kernel(where_ref, book_ref, table_ref):
    item = where_ref[0]
    low = item & 7
    picked = jnp.concatenate(
        [
            book_ref[0, item],
            book_ref[0, (item + 1) & 15],
            book_ref[1, 2 * low],
            book_ref[1, 2 * low + 1],
            book_ref[2].reshape(256, DS),
            book_ref[3].reshape(256, DS),
        ],
        axis=0,
    )
    table_ref[...] = picked.astype(F32).T.astype(BF16)


def cross_kernel(where_ref, packed_ref, teacher_ref, table_ref, keep_ref, send_ref, student_ref, tnorm_ref, inv_ref, packed):
    packed[...] = packed_ref[...].astype(F32)
    item, feat, me = where_ref[0], where_ref[1], where_ref[2]
    low = item & 7
    table = table_ref[...]
    per = CHUNK // 128
    small = lax.broadcasted_iota(jnp.int32, (32, CHUNK), 0)
    large = lax.broadcasted_iota(jnp.int32, (256, CHUNK), 0)
    for n in range(2048 // CHUNK):
        first = (codes_of(packed, 0, n * per, per) - 16 * item) & 255
        second = codes_of(packed, 1, n * per, per) - 32 * low
        onehot = jnp.concatenate(
            [
                (small == first).astype(F32),
                (small == second).astype(F32),
                (large == codes_of(packed, 2, n * per, per)).astype(F32),
                (large == codes_of(packed, 3, n * per, per)).astype(F32),
            ],
            axis=0,
        ).astype(BF16)
        recon = jnp.dot(table, onehot, preferred_element_type=F32)
        inv = lax.rsqrt(jnp.sum(recon * recon, axis=0, keepdims=True) / DS + EPS)
        student_ref[:, n * CHUNK : (n + 1) * CHUNK] = (recon * inv).astype(BF16)
        inv_ref[:, n * CHUNK : (n + 1) * CHUNK] = inv
    squares = packed[0, 0:16, :]
    for j in range(1, 16):
        squares = squares + packed[j, 0:16, :]
    factor = lax.rsqrt(squares / DT + EPS)
    for j in range(16):
        column = jnp.broadcast_to(factor[j : j + 1, :], (128, 128)).T
        rows = teacher_ref[j * 128 : (j + 1) * 128, :].astype(F32)
        tnorm_ref[j * 128 : (j + 1) * 128, :] = (rows * jnp.concatenate([column, column], axis=1)).astype(BF16)
    student = student_ref[...]
    cross = jnp.dot(student, tnorm_ref[...], preferred_element_type=F32)
    mine = student_ref[pl.ds(pl.multiple_of(feat * 32, 32), 32), :]
    gram = lax.dot_general(mine, student, NT, preferred_element_type=F32)
    for b in range(4):
        to = b ^ me

        def store(ref, at):
            ref[at, 0:128, :] = cross[b * 128 : (b + 1) * 128, 0:128].astype(ref.dtype)
            ref[at, 128:256, :] = cross[b * 128 : (b + 1) * 128, 128:256].astype(ref.dtype)
            ref[at, 256:288, :] = gram[:, b * 128 : (b + 1) * 128].astype(ref.dtype)

        @pl.when(to < 2)
        def _():
            store(keep_ref, to)

        @pl.when(to >= 2)
        def _():
            store(send_ref, to - 2)


def grad_kernel(where_ref, packed_ref, whole_ref, student_ref, tnorm_ref, inv_ref, keep_ref, send_ref, loss_ref, cross, gram, packed, grads, onehots):
    packed[...] = packed_ref[...].astype(F32)
    item, feat, me = where_ref[0], where_ref[1], where_ref[2]
    place, zb, half, kept = where_ref[3], where_ref[4], where_ref[5], where_ref[6]
    for b in range(4):
        block = whole_ref[b ^ me]
        cross[b * 128 : (b + 1) * 128, 0:128] = block[0:128]
        cross[b * 128 : (b + 1) * 128, 128:256] = block[128:256]
        gram[:, b * 128 : (b + 1) * 128] = block[256:288]
    cross_f = cross[...].astype(F32)
    gram_f = gram[...].astype(F32)
    loss = jnp.sum(gram_f * gram_f, keepdims=True) - 2.0 * jnp.sum(cross_f * cross_f, keepdims=True)
    high = loss.astype(BF16).astype(F32)
    middle = (loss - high).astype(BF16).astype(F32)
    rest = (loss - high - middle).astype(BF16).astype(F32)
    row = lax.broadcasted_iota(jnp.int32, (8, DS), 0)
    lane = lax.broadcasted_iota(jnp.int32, (8, DS), 1)
    parts = jnp.where(row == 0, high, jnp.where(row == 1, middle, jnp.where(row == 2, rest, 0.0)))
    loss_ref[...] = jnp.where(lane == feat, parts, 0.0)
    gram_t = gram_f.T.astype(BF16)
    per = CHUNK // 128
    large = lax.broadcasted_iota(jnp.int32, (512, CHUNK), 0)
    small = lax.broadcasted_iota(jnp.int32, (64, CHUNK), 0) + 512
    for n in range(2048 // CHUNK):
        span = slice(n * CHUNK, (n + 1) * CHUNK)
        mine = student_ref[pl.ds(pl.multiple_of(feat * 32, 32), 32), span]
        push = jnp.dot(gram_t, mine, preferred_element_type=F32)
        pull = lax.dot_general(cross[...], tnorm_ref[span, :], NT, preferred_element_type=F32)
        value = push - pull
        student = student_ref[:, span].astype(F32)
        mean = jnp.sum(value * student, axis=0, keepdims=True) / DS
        grads[:, span] = ((value - student * mean) * (inv_ref[:, span] / 32768.0)).astype(BF16)

        def spot(code, level):
            low = code & 15
            return (((code >> 4) ^ place) << 5) + (((low >> 3) ^ zb) << 4) + 8 * level + (low & 7)

        first = (codes_of(packed, 0, n * per, per) - 16 * item) & 255
        own = 512 + ((first >> 3) ^ kept) * 24 + (first & 7)
        first = jnp.where(first < 16, own, 560)
        second = codes_of(packed, 1, n * per, per) - 32 * (item & 7)
        low = second & 15
        second = 520 + ((low >> 3) ^ kept) * 24 + ((second >> 4) ^ half) * 8 + (low & 7)
        third = spot(codes_of(packed, 2, n * per, per), 0)
        fourth = spot(codes_of(packed, 3, n * per, per), 1)
        onehots[0:512, span] = ((large == third) | (large == fourth)).astype(F32).astype(BF16)
        onehots[512:576, span] = ((small == first) | (small == second)).astype(F32).astype(BF16)
    total = lax.dot_general(onehots[...], grads[...], NT, preferred_element_type=F32)
    for k, ref in enumerate((keep_ref, send_ref)):
        ref[0:32] = total[k * 256 : (k + 1) * 256].reshape(32, 8, DS).astype(ref.dtype)
        ref[32:35] = total[512 + k * 24 : 536 + k * 24].reshape(3, 8, DS).astype(ref.dtype)
        ref[35] = total[560:568].astype(ref.dtype)


def spread(c, x, where_ref, piece_ref, out_hbm, rows, sems):
    place, zb = where_ref[3], where_ref[4]
    base = (c * 8 + x * 4) ^ (place & 12)
    kept, axl = base >> 3, (base >> 2) & 1
    copies = []

    def copy(level, start, count, to):
        target = out_hbm.at[level, pl.ds(pl.multiple_of(to, 8), count)]
        copies.append(pltpu.make_async_copy(rows.at[level, pl.ds(start, count)], target, sems.at[len(copies)]))
        copies[-1].start()

    for k, level in enumerate((2, 3, 0, 1)):
        for y in range(4):
            for z in range(2):
                at = pl.multiple_of((y ^ (place & 3)) * 16 + (z ^ zb) * 8, 8)
                rows[level, pl.ds(at, 8), :] = piece_ref[y, z, k].astype(F32)
        if level > 1:
            copy(level, 0, 64, base * 16)
            continue
        for j in range(8):
            ay, ac = j >> 1, j & 1
            if level == 0:
                row = (ay * 4 + axl * 2 + ac) * 16
            else:
                row = ((ay & 1) * 4 + axl * 2 + ac) * 32 + (ay >> 1) * 16
            copy(level, j * 8, 8, row + kept * 8)
    for one in copies:
        one.wait()


def first_kernel(where_ref, piece_ref, parts_ref, out_hbm, loss_ref, rows, sems):
    loss_ref[...] = jnp.sum(parts_ref[...], keepdims=True) / (32768.0 * 32768.0 * DS)
    spread(0, 0, where_ref, piece_ref, out_hbm, rows, sems)


def next_kernel(c, x):
    def kernel(where_ref, piece_ref, begun_hbm, out_hbm, *refs):
        *token, rows, sems = refs
        if token:
            token[0][...] = jnp.zeros((8, DS), BF16)
        spread(c, x, where_ref, piece_ref, out_hbm, rows, sems)

    return kernel


def call(kernel, ins, outs, scratch=(), aliases=None):
    return pl.pallas_call(
        kernel,
        out_shape=[jax.ShapeDtypeStruct(shape, kind) for shape, kind, _ in outs],
        in_specs=[pl.BlockSpec(memory_space=space) for space in ins],
        out_specs=[pl.BlockSpec(memory_space=space) for _, _, space in outs],
        scratch_shapes=list(scratch),
        input_output_aliases=aliases or {},
        compiler_params=pltpu.CompilerParams(vmem_limit_bytes=48 << 20),
    )


def swap(array, axis, size, bit):
    return lax.ppermute(array, axis, [(j, j ^ bit) for j in range(size)])


def in_hbm(array):
    return pltpu.with_memory_space_constraint(array, pltpu.HBM)


def across_x(array):
    return swap(array, ("xl", "c"), 4, 3)


def across_y(array, bits):
    return swap(array, ("y", "c"), 8, 2 * bits + (bits & 1))


def across_z(array):
    return swap(array, ("c", "zb"), 4, 3)


def on_device(teacher, codebooks, codes):
    y, xl, c = lax.axis_index("y"), lax.axis_index("xl"), lax.axis_index("c")
    zb = lax.axis_index("zb")
    item = y * 4 + xl * 2 + c
    feat = lax.axis_index(FEAT)
    kept = c ^ xl ^ (y & 1) ^ lax.axis_index("xh") ^ (lax.axis_index("za") & 1) ^ zb
    where = jnp.stack([item, feat, kept * 2 + xl, kept * 8 + xl * 4 + y, zb, y >> 1, kept]).astype(jnp.int32)

    teacher, packed = call(
        pack_kernel,
        [HBM, HBM],
        [((2048, 256), BF16, VMEM), ((24, 128), BF16, VMEM)],
        [pltpu.VMEM((4, 128), jnp.int32), pltpu.VMEM((24, 128), F32), pltpu.SemaphoreType.DMA((5,))],
    )(in_hbm(teacher), in_hbm(codes.T))
    packed = lax.all_to_all(jnp.broadcast_to(packed[None], (16, 24, 128)), FEAT, 0, 0, tiled=True)
    (table,) = call(table_kernel, [SMEM, VMEM], [((DS, ROWS), BF16, VMEM)])(where, codebooks.reshape(4, 16, 16, DS))

    keep, send, student, tnorm, inv = call(
        cross_kernel,
        [SMEM, VMEM, VMEM, VMEM],
        [
            ((2, 288, 128), F32, VMEM),
            ((2, 288, 128), BF16, VMEM),
            ((DS, 2048), BF16, VMEM),
            ((2048, 256), BF16, VMEM),
            ((1, 2048), F32, VMEM),
        ],
        [pltpu.VMEM((16, 24, 128), F32)],
    )(where, packed, teacher, table)

    part = keep + swap(send, "c", 2, 1).astype(F32)
    part = part[0] + across_x(part[1].astype(BF16)).astype(F32)
    own = part.astype(BF16)
    a, b, d = (across_y(own, k) for k in (1, 2, 3))
    whole = ((own.astype(F32) + a.astype(F32)) + (b.astype(F32) + d.astype(F32))).astype(BF16)
    whole = jnp.stack([whole, across_x(whole)])
    whole = jnp.concatenate([whole, swap(whole, "c", 2, 1)])

    keep, send, loss = call(
        grad_kernel,
        [SMEM] + [VMEM] * 5,
        [((36, 8, DS), F32, VMEM), ((36, 8, DS), BF16, VMEM), ((8, DS), F32, VMEM)],
        [
            pltpu.VMEM((DS, 256), BF16),
            pltpu.VMEM((32, DS), BF16),
            pltpu.VMEM((16, 24, 128), F32),
            pltpu.VMEM((DS, 2048), BF16),
            pltpu.VMEM((ROWS, 2048), BF16),
        ],
    )(where, packed, whole, student, tnorm, inv)

    got = swap(send, "c", 2, 1).astype(F32)
    sums = keep[:32] + got[:32]
    low = jnp.where(c == 0, keep[32:], got[32:])
    high = jnp.where(c == 0, got[32:], keep[32:])
    holds = kept == 0
    none = jnp.zeros((), BF16)
    high_zero = high[0] + jnp.where(holds, low[3], 0.0)
    ahead = jnp.where(holds, high[3:], 0.0).astype(BF16)
    got = across_x(jnp.concatenate([sums[16:].astype(BF16), ahead]))
    sums = sums[:16] + got[:16].astype(F32)
    low_zero = low[0] + jnp.where(xl == 1, got[16].astype(F32), 0.0)
    ahead = jnp.where(xl == 0, got[16:], none)
    odd = (y & 1) == 1
    one = across_y(jnp.concatenate([sums[4:8].astype(BF16), jnp.where(odd, none, ahead)]), 1)
    two = across_y(jnp.concatenate([sums[8:12], low[2:3], high[2:3]]).astype(BF16), 2)
    three = across_y(jnp.concatenate([sums[12:16].astype(BF16), jnp.where(odd, ahead, none)]), 3)
    sums = sums[0:4] + one[:4].astype(F32) + two[:4].astype(F32) + three[:4].astype(F32)
    low = jnp.stack([low_zero + one[4].astype(F32) + three[4].astype(F32), low[1] + two[4].astype(F32)])
    high = jnp.stack([high_zero, high[1] + two[5].astype(F32)])

    sent = jnp.concatenate([sums[2:4], jnp.where(zb == 0, high, low), loss[None]]).astype(BF16)
    rows = jnp.concatenate([sums[0:2], jnp.where(zb == 0, low, high), loss[None]]) + across_z(sent).astype(F32)
    own = (rows + swap(rows, ("c", "xh"), 4, 3)).astype(BF16)
    a, b, d = (swap(own, ("c", "za"), 8, k + 4 * (k & 1)).astype(F32) for k in (1, 2, 3))
    rows = (own.astype(F32) + a) + (b + d)
    loss = rows[4]
    rows = rows[:4].astype(BF16)

    rows = jnp.stack([rows, across_z(rows)])
    rows = jnp.stack([rows] + [across_y(rows, k) for k in (1, 2, 3)])
    parts = across_x(rows[:2]), swap(rows[2:], ("xl", "xh"), 4, 3)
    far = swap(rows, "c", 2, 1)
    rows_and_sems = [pltpu.VMEM((4, 64, DS), F32), pltpu.SemaphoreType.DMA((18,))]
    out = ((4, 256, DS), F32, ANY)
    outs = [out, ((8, DS), BF16, VMEM)]
    grads, loss = call(first_kernel, [SMEM, VMEM, VMEM], [out, ((1, 1), F32, VMEM)], rows_and_sems)(where, rows, loss)
    grads, token = call(next_kernel(1, 0), [SMEM, VMEM, ANY], outs, rows_and_sems, {2: 0})(where, far, grads)
    beside = jnp.concatenate([part + token for part in parts])
    far_beside = swap(beside, "c", 2, 1)
    for c, piece in ((0, beside), (1, far_beside)):
        (grads,) = call(next_kernel(c, 1), [SMEM, VMEM, ANY], [out], rows_and_sems, {2: 0})(where, piece, grads)
    return (loss.reshape(()), grads)


def solution(mesh):
    split = Mesh(mesh.devices.reshape(4, 2, 2, 2, 4, 2), ITEM + FEAT)
    return jax.shard_map(
        on_device,
        mesh=split,
        in_specs=(P(ITEM, FEAT), P(), P(ITEM + FEAT, None)),
        out_specs=(P(), P()),
        check_vma=False,
    )
```

```python
import jax
import jax.numpy as jnp
from jax import lax
from jax.experimental import pallas as pl
from jax.experimental.pallas import tpu as pltpu
from jax.sharding import Mesh
from jax.sharding import PartitionSpec as P

DT = 4096
DS = 512
EPS = 1e-06
F32 = jnp.float32
BF16 = jnp.bfloat16
FEAT = ("xh", "za", "zb")
ITEM = ("y", "xl", "c")
ROWS = 576
CHUNK = 512

NT = (((1,), (1,)), ((), ()))
ANY, HBM, SMEM, VMEM = pl.ANY, pltpu.HBM, pltpu.SMEM, pltpu.VMEM


def lanes_of(packed_ref, row, start, count):
    return jnp.concatenate([packed_ref[start + j, row : row + 1, :] for j in range(count)], axis=1)


def codes_of(packed_ref, level, start, count):
    return lanes_of(packed_ref, 16 + level, start, count).astype(jnp.int32)


def pack_kernel(teacher_hbm, codes_hbm, teacher_ref, packed_ref, codes_ref, gathered, sems):
    first = pltpu.make_async_copy(codes_hbm, codes_ref, sems.at[4])
    first.start()
    copies = []
    for n in range(4):
        rows = pl.ds(n * 512, 512)
        copies.append(pltpu.make_async_copy(teacher_hbm.at[rows], teacher_ref.at[rows], sems.at[n]))
        copies[-1].start()
    first.wait()
    gathered[16:20, :] = codes_ref[...].astype(F32)
    gathered[20:24, :] = jnp.zeros((4, 128), F32)
    ones = jnp.ones((8, 256), BF16)
    for n in range(4):
        copies[n].wait()
        rows = teacher_ref[n * 512 : (n + 1) * 512, :].astype(F32)
        squares = rows * rows
        upper = squares.astype(BF16)
        lower = (squares - upper.astype(F32)).astype(BF16)
        sums = lax.dot_general(ones, upper, NT, preferred_element_type=F32)
        sums = sums + lax.dot_general(ones, lower, NT, preferred_element_type=F32)
        for j in range(4):
            gathered[4 * n + j : 4 * n + j + 1, :] = sums[0:1, j * 128 : (j + 1) * 128]
    packed_ref[...] = gathered[...].astype(BF16)


def table_kernel(where_ref, book_ref, table_ref):
    item = where_ref[0]
    low = item & 7
    picked = jnp.concatenate(
        [
            book_ref[0, item],
            book_ref[0, (item + 1) & 15],
            book_ref[1, 2 * low],
            book_ref[1, 2 * low + 1],
            book_ref[2].reshape(256, DS),
            book_ref[3].reshape(256, DS),
        ],
        axis=0,
    )
    table_ref[...] = picked.astype(F32).T.astype(BF16)


def cross_kernel(where_ref, packed_ref, teacher_ref, table_ref, keep_ref, send_ref, student_ref, tnorm_ref, inv_ref, packed):
    packed[...] = packed_ref[...].astype(F32)
    item, feat, me = where_ref[0], where_ref[1], where_ref[2]
    low = item & 7
    table = table_ref[...]
    per = CHUNK // 128
    small = lax.broadcasted_iota(jnp.int32, (32, CHUNK), 0)
    large = lax.broadcasted_iota(jnp.int32, (256, CHUNK), 0)
    for n in range(2048 // CHUNK):
        first = (codes_of(packed, 0, n * per, per) - 16 * item) & 255
        second = codes_of(packed, 1, n * per, per) - 32 * low
        onehot = jnp.concatenate(
            [
                (small == first).astype(F32),
                (small == second).astype(F32),
                (large == codes_of(packed, 2, n * per, per)).astype(F32),
                (large == codes_of(packed, 3, n * per, per)).astype(F32),
            ],
            axis=0,
        ).astype(BF16)
        recon = jnp.dot(table, onehot, preferred_element_type=F32)
        inv = lax.rsqrt(jnp.sum(recon * recon, axis=0, keepdims=True) / DS + EPS)
        student_ref[:, n * CHUNK : (n + 1) * CHUNK] = (recon * inv).astype(BF16)
        inv_ref[:, n * CHUNK : (n + 1) * CHUNK] = inv
    squares = packed[0, 0:16, :]
    for j in range(1, 16):
        squares = squares + packed[j, 0:16, :]
    factor = lax.rsqrt(squares / DT + EPS)
    for j in range(16):
        column = jnp.broadcast_to(factor[j : j + 1, :], (128, 128)).T
        rows = teacher_ref[j * 128 : (j + 1) * 128, :].astype(F32)
        tnorm_ref[j * 128 : (j + 1) * 128, :] = (rows * jnp.concatenate([column, column], axis=1)).astype(BF16)
    student = student_ref[...]
    cross = jnp.dot(student, tnorm_ref[...], preferred_element_type=F32)
    mine = student_ref[pl.ds(pl.multiple_of(feat * 32, 32), 32), :]
    gram = lax.dot_general(mine, student, NT, preferred_element_type=F32)
    for b in range(4):
        to = b ^ me

        def store(ref, at):
            ref[at, 0:128, :] = cross[b * 128 : (b + 1) * 128, 0:128].astype(ref.dtype)
            ref[at, 128:256, :] = cross[b * 128 : (b + 1) * 128, 128:256].astype(ref.dtype)
            ref[at, 256:288, :] = gram[:, b * 128 : (b + 1) * 128].astype(ref.dtype)

        @pl.when(to < 2)
        def _():
            store(keep_ref, to)

        @pl.when(to >= 2)
        def _():
            store(send_ref, to - 2)


def grad_kernel(where_ref, packed_ref, whole_ref, student_ref, tnorm_ref, inv_ref, keep_ref, send_ref, loss_ref, cross, gram, packed, grads, onehots):
    packed[...] = packed_ref[...].astype(F32)
    item, feat, me = where_ref[0], where_ref[1], where_ref[2]
    place, zb, half, kept = where_ref[3], where_ref[4], where_ref[5], where_ref[6]
    for b in range(4):
        block = whole_ref[b ^ me]
        cross[b * 128 : (b + 1) * 128, 0:128] = block[0:128]
        cross[b * 128 : (b + 1) * 128, 128:256] = block[128:256]
        gram[:, b * 128 : (b + 1) * 128] = block[256:288]
    cross_f = cross[...].astype(F32)
    gram_f = gram[...].astype(F32)
    loss = jnp.sum(gram_f * gram_f, keepdims=True) - 2.0 * jnp.sum(cross_f * cross_f, keepdims=True)
    high = loss.astype(BF16).astype(F32)
    middle = (loss - high).astype(BF16).astype(F32)
    rest = (loss - high - middle).astype(BF16).astype(F32)
    row = lax.broadcasted_iota(jnp.int32, (8, DS), 0)
    lane = lax.broadcasted_iota(jnp.int32, (8, DS), 1)
    parts = jnp.where(row == 0, high, jnp.where(row == 1, middle, jnp.where(row == 2, rest, 0.0)))
    loss_ref[...] = jnp.where(lane == feat, parts, 0.0)
    gram_t = gram_f.T.astype(BF16)
    per = CHUNK // 128
    large = lax.broadcasted_iota(jnp.int32, (512, CHUNK), 0)
    small = lax.broadcasted_iota(jnp.int32, (64, CHUNK), 0) + 512
    for n in range(2048 // CHUNK):
        span = slice(n * CHUNK, (n + 1) * CHUNK)
        mine = student_ref[pl.ds(pl.multiple_of(feat * 32, 32), 32), span]
        push = jnp.dot(gram_t, mine, preferred_element_type=F32)
        pull = lax.dot_general(cross[...], tnorm_ref[span, :], NT, preferred_element_type=F32)
        value = push - pull
        student = student_ref[:, span].astype(F32)
        mean = jnp.sum(value * student, axis=0, keepdims=True) / DS
        grads[:, span] = ((value - student * mean) * (inv_ref[:, span] / 32768.0)).astype(BF16)

        def spot(code, level):
            low = code & 15
            return (((code >> 4) ^ place) << 5) + (((low >> 3) ^ zb) << 4) + 8 * level + (low & 7)

        first = (codes_of(packed, 0, n * per, per) - 16 * item) & 255
        own = 512 + ((first >> 3) ^ kept) * 24 + (first & 7)
        first = jnp.where(first < 16, own, 560)
        second = codes_of(packed, 1, n * per, per) - 32 * (item & 7)
        low = second & 15
        second = 520 + ((low >> 3) ^ kept) * 24 + ((second >> 4) ^ half) * 8 + (low & 7)
        third = spot(codes_of(packed, 2, n * per, per), 0)
        fourth = spot(codes_of(packed, 3, n * per, per), 1)
        onehots[0:512, span] = ((large == third) | (large == fourth)).astype(F32).astype(BF16)
        onehots[512:576, span] = ((small == first) | (small == second)).astype(F32).astype(BF16)
    total = lax.dot_general(onehots[...], grads[...], NT, preferred_element_type=F32)
    for k, ref in enumerate((keep_ref, send_ref)):
        ref[0:32] = total[k * 256 : (k + 1) * 256].reshape(32, 8, DS).astype(ref.dtype)
        ref[32:35] = total[512 + k * 24 : 536 + k * 24].reshape(3, 8, DS).astype(ref.dtype)
        ref[35] = total[560:568].astype(ref.dtype)


def spread(c, x, where_ref, piece_ref, out_hbm, rows, sems):
    place, zb = where_ref[3], where_ref[4]
    base = (c * 8 + x * 4) ^ (place & 12)
    kept, axl = base >> 3, (base >> 2) & 1
    copies = []

    def copy(level, start, count, to):
        target = out_hbm.at[level, pl.ds(pl.multiple_of(to, 8), count)]
        copies.append(pltpu.make_async_copy(rows.at[level, pl.ds(start, count)], target, sems.at[len(copies)]))
        copies[-1].start()

    for k, level in enumerate((2, 3, 0, 1)):
        for y in range(4):
            for z in range(2):
                at = pl.multiple_of((y ^ (place & 3)) * 16 + (z ^ zb) * 8, 8)
                rows[level, pl.ds(at, 8), :] = piece_ref[y, z, k].astype(F32)
        if level > 1:
            copy(level, 0, 64, base * 16)
            continue
        for j in range(8):
            ay, ac = j >> 1, j & 1
            if level == 0:
                row = (ay * 4 + axl * 2 + ac) * 16
            else:
                row = ((ay & 1) * 4 + axl * 2 + ac) * 32 + (ay >> 1) * 16
            copy(level, j * 8, 8, row + kept * 8)
    for one in copies:
        one.wait()


def first_kernel(where_ref, piece_ref, parts_ref, out_hbm, loss_ref, rows, sems):
    loss_ref[...] = jnp.sum(parts_ref[...], keepdims=True) / (32768.0 * 32768.0 * DS)
    spread(0, 0, where_ref, piece_ref, out_hbm, rows, sems)


def next_kernel(c, x):
    def kernel(where_ref, piece_ref, begun_hbm, out_hbm, *refs):
        *token, rows, sems = refs
        if token:
            token[0][...] = jnp.zeros((8, DS), BF16)
        spread(c, x, where_ref, piece_ref, out_hbm, rows, sems)

    return kernel


def call(kernel, ins, outs, scratch=(), aliases=None):
    return pl.pallas_call(
        kernel,
        out_shape=[jax.ShapeDtypeStruct(shape, kind) for shape, kind, _ in outs],
        in_specs=[pl.BlockSpec(memory_space=space) for space in ins],
        out_specs=[pl.BlockSpec(memory_space=space) for _, _, space in outs],
        scratch_shapes=list(scratch),
        input_output_aliases=aliases or {},
        compiler_params=pltpu.CompilerParams(vmem_limit_bytes=48 << 20),
    )


def swap(array, axis, size, bit):
    return lax.ppermute(array, axis, [(j, j ^ bit) for j in range(size)])


def in_hbm(array):
    return pltpu.with_memory_space_constraint(array, pltpu.HBM)


def across_x(array):
    return swap(array, ("xl", "c"), 4, 3)


def across_y(array, bits):
    return swap(array, ("y", "c"), 8, 2 * bits + (bits & 1))


def across_z(array):
    return swap(array, ("c", "zb"), 4, 3)


def on_device(teacher, codebooks, codes):
    y, xl, c = lax.axis_index("y"), lax.axis_index("xl"), lax.axis_index("c")
    zb = lax.axis_index("zb")
    item = y * 4 + xl * 2 + c
    feat = lax.axis_index(FEAT)
    kept = c ^ xl ^ (y & 1) ^ lax.axis_index("xh") ^ (lax.axis_index("za") & 1) ^ zb
    where = jnp.stack([item, feat, kept * 2 + xl, kept * 8 + xl * 4 + y, zb, y >> 1, kept]).astype(jnp.int32)

    teacher, packed = call(
        pack_kernel,
        [HBM, HBM],
        [((2048, 256), BF16, VMEM), ((24, 128), BF16, VMEM)],
        [pltpu.VMEM((4, 128), jnp.int32), pltpu.VMEM((24, 128), F32), pltpu.SemaphoreType.DMA((5,))],
    )(in_hbm(teacher), in_hbm(codes.T))
    packed = lax.all_to_all(jnp.broadcast_to(packed[None], (16, 24, 128)), FEAT, 0, 0, tiled=True)
    (table,) = call(table_kernel, [SMEM, VMEM], [((DS, ROWS), BF16, VMEM)])(where, codebooks.reshape(4, 16, 16, DS))

    keep, send, student, tnorm, inv = call(
        cross_kernel,
        [SMEM, VMEM, VMEM, VMEM],
        [
            ((2, 288, 128), F32, VMEM),
            ((2, 288, 128), BF16, VMEM),
            ((DS, 2048), BF16, VMEM),
            ((2048, 256), BF16, VMEM),
            ((1, 2048), F32, VMEM),
        ],
        [pltpu.VMEM((16, 24, 128), F32)],
    )(where, packed, teacher, table)

    part = keep + swap(send, "c", 2, 1).astype(F32)
    part = part[0] + across_x(part[1].astype(BF16)).astype(F32)
    own = part.astype(BF16)
    a, b, d = (across_y(own, k) for k in (1, 2, 3))
    whole = ((own.astype(F32) + a.astype(F32)) + (b.astype(F32) + d.astype(F32))).astype(BF16)
    whole = jnp.stack([whole, across_x(whole)])
    whole = jnp.concatenate([whole, swap(whole, "c", 2, 1)])

    keep, send, loss = call(
        grad_kernel,
        [SMEM] + [VMEM] * 5,
        [((36, 8, DS), F32, VMEM), ((36, 8, DS), BF16, VMEM), ((8, DS), F32, VMEM)],
        [
            pltpu.VMEM((DS, 256), BF16),
            pltpu.VMEM((32, DS), BF16),
            pltpu.VMEM((16, 24, 128), F32),
            pltpu.VMEM((DS, 2048), BF16),
            pltpu.VMEM((ROWS, 2048), BF16),
        ],
    )(where, packed, whole, student, tnorm, inv)

    got = swap(send, "c", 2, 1).astype(F32)
    sums = keep[:32] + got[:32]
    low = jnp.where(c == 0, keep[32:], got[32:])
    high = jnp.where(c == 0, got[32:], keep[32:])
    holds = kept == 0
    none = jnp.zeros((), BF16)
    high_zero = high[0] + jnp.where(holds, low[3], 0.0)
    ahead = jnp.where(holds, high[3:], 0.0).astype(BF16)
    got = across_x(jnp.concatenate([sums[16:].astype(BF16), ahead]))
    sums = sums[:16] + got[:16].astype(F32)
    low_zero = low[0] + jnp.where(xl == 1, got[16].astype(F32), 0.0)
    ahead = jnp.where(xl == 0, got[16:], none)
    odd = (y & 1) == 1
    one = across_y(jnp.concatenate([sums[4:8].astype(BF16), jnp.where(odd, none, ahead)]), 1)
    two = across_y(jnp.concatenate([sums[8:12], low[2:3], high[2:3]]).astype(BF16), 2)
    three = across_y(jnp.concatenate([sums[12:16].astype(BF16), jnp.where(odd, ahead, none)]), 3)
    sums = sums[0:4] + one[:4].astype(F32) + two[:4].astype(F32) + three[:4].astype(F32)
    low = jnp.stack([low_zero + one[4].astype(F32) + three[4].astype(F32), low[1] + two[4].astype(F32)])
    high = jnp.stack([high_zero, high[1] + two[5].astype(F32)])

    sent = jnp.concatenate([sums[2:4], jnp.where(zb == 0, high, low), loss[None]]).astype(BF16)
    own = jnp.concatenate([sums[0:2], jnp.where(zb == 0, low, high), loss[None]]).astype(BF16)
    a = swap(own, ("c", "xh"), 4, 3).astype(F32)
    b = swap(sent, ("xh", "zb"), 4, 3).astype(F32)
    d = across_z(sent).astype(F32)
    own = ((own.astype(F32) + d) + (a + b)).astype(BF16)
    a, b, d = (swap(own, ("c", "za"), 8, k + 4 * (k & 1)).astype(F32) for k in (1, 2, 3))
    rows = (own.astype(F32) + a) + (b + d)
    loss = rows[4]
    rows = rows[:4].astype(BF16)

    rows = jnp.stack([rows, across_z(rows)])
    rows = jnp.stack([rows] + [across_y(rows, k) for k in (1, 2, 3)])
    parts = across_x(rows[:2]), swap(rows[2:], ("xl", "xh"), 4, 3)
    far = swap(rows, "c", 2, 1)
    rows_and_sems = [pltpu.VMEM((4, 64, DS), F32), pltpu.SemaphoreType.DMA((18,))]
    out = ((4, 256, DS), F32, ANY)
    outs = [out, ((8, DS), BF16, VMEM)]
    grads, loss = call(first_kernel, [SMEM, VMEM, VMEM], [out, ((1, 1), F32, VMEM)], rows_and_sems)(where, rows, loss)
    grads, token = call(next_kernel(1, 0), [SMEM, VMEM, ANY], outs, rows_and_sems, {2: 0})(where, far, grads)
    beside = jnp.concatenate([part + token for part in parts])
    far_beside = swap(beside, "c", 2, 1)
    for c, piece in ((0, beside), (1, far_beside)):
        (grads,) = call(next_kernel(c, 1), [SMEM, VMEM, ANY], [out], rows_and_sems, {2: 0})(where, piece, grads)
    return (loss.reshape(()), grads)


def solution(mesh):
    split = Mesh(mesh.devices.reshape(4, 2, 2, 2, 4, 2), ITEM + FEAT)
    return jax.shard_map(
        on_device,
        mesh=split,
        in_specs=(P(ITEM, FEAT), P(), P(ITEM + FEAT, None)),
        out_specs=(P(), P()),
        check_vma=False,
    )
```
